32 devices in a mesh: seq: 4 (over y, x), vocab: 8 (over z, core).
Axes of the slice: x: 2, y: 2, z: 4, core: 2. Of those that a mesh axis runs over, the one named last changes fastest.
Arguments:
- teacher_hidden: bfloat16 [1024, 8192], P(None, 'seq'), may hold values from -480 to 480
- teacher_head: bfloat16 [8192, 81920], P('seq', 'vocab'), may hold values from -1 to 1
- student_hidden: bfloat16 [1024, 3584], P(None, 'seq'), may hold values from -480 to 480
- student_head: bfloat16 [3584, 81920], P('seq', 'vocab'), may hold values from -1 to 1
- kept: int32 [8, 64], replicated, may hold values from 0 to 639, as said below
Outputs:
- loss_rows: float32 [1024], P('seq')
- hidden_grad: bfloat16 [1024, 3584], P('vocab', 'seq')
- head_grad: bfloat16 [3584, 81920], P('seq', 'vocab')
The draws below stay inside these ranges and needn't reach their ends.
Inputs may be any that keep to these rules, and one draw needn't show every extreme that they name: `kept`: each row holds 64 distinct block ids in ascending order. In every row at most 8 of them lie within one run of 80 consecutive blocks starting at a multiple of 80, and in every row some such run holds exactly 8.
All inputs are finite; a program needn't handle non-finite values.
Results may differ from the reference program's by a relative error of at most 0.0049.
Values may be sent and summed in bfloat16 or wider, within the bound.
A program may use at most 256 MiB of HBM per device.

```python
import jax
import jax.numpy as jnp
from jax import lax

DT = 8192
DS = 3584
VOCAB = 81920
BLOCK = 128
KEPT = 64
TOKENS = 1024
ROW_BLOCK_TOTAL = 8
NBLOCKS = 640
NB_DEV = 80
MOSTB = 8


def head_block(head_key, number, depth):
    values = jnp.clip(jax.random.normal(jax.random.fold_in(head_key, number), (depth, BLOCK), jnp.float32), -4.0, 4.0)
    values = values * (1.0 / float(depth) ** 0.5)
    return values.astype(jnp.bfloat16).astype(jnp.float32)


def whole_head(head_key, depth):
    blocks = jax.vmap(lambda number: head_block(head_key, number, depth))(jnp.arange(NBLOCKS, dtype=jnp.int32))
    return jnp.transpose(blocks, (1, 0, 2)).reshape(depth, VOCAB)


def scaled_rows(key, depth):
    values = jnp.clip(jax.random.normal(jax.random.fold_in(key, 3), (TOKENS, depth), jnp.float32), -6.0, 6.0)
    return values


def draw_teacher_head(key, part):
    return whole_head(jax.random.fold_in(key, 31), DT).astype(jnp.bfloat16)


def draw_student_head(key, part):
    return whole_head(jax.random.fold_in(key, 37), DS).astype(jnp.bfloat16)


def draw_teacher_hidden(key, part):
    return scaled_rows(jax.random.fold_in(key, 11), DT).astype(jnp.bfloat16)


def draw_student_hidden(key, part):
    return scaled_rows(jax.random.fold_in(key, 23), DS).astype(jnp.bfloat16)


def draw_kept(key, part):
    device_shards = NBLOCKS // NB_DEV
    slot_entries = device_shards * MOSTB
    random_keys = jax.random.split(jax.random.fold_in(key, 7), 4)
    extra_boost = jax.random.randint(random_keys[0], (ROW_BLOCK_TOTAL, device_shards), 0, 3)
    forced_pick = jax.random.randint(random_keys[1], (ROW_BLOCK_TOTAL,), 0, device_shards)
    extra_boost = jnp.where(jnp.arange(device_shards)[None, :] == forced_pick[:, None], 3, extra_boost)
    random_noise = jax.random.randint(random_keys[2], (ROW_BLOCK_TOTAL, device_shards, MOSTB), 0, 1024)
    primary_choice = (extra_boost[:, :, None] * 1024 + random_noise).reshape(ROW_BLOCK_TOTAL, slot_entries)
    scores = primary_choice * slot_entries + jnp.arange(slot_entries)[None, :]
    unused, chosen = lax.top_k(scores, KEPT)
    shard_of = chosen // MOSTB
    slot_of = chosen % MOSTB
    offsets = jax.random.randint(random_keys[3], (ROW_BLOCK_TOTAL, device_shards), 0, NB_DEV)
    shift_of = jnp.take_along_axis(offsets, shard_of, axis=1)
    block_of = shard_of * NB_DEV + (shift_of + slot_of) % NB_DEV
    return jnp.sort(block_of, axis=1).astype(jnp.int32)


def setup_inputs(seed: int = 0) -> dict:
    keys = jax.random.split(jax.random.key(seed), 6)
    teacher_hidden = draw_teacher_hidden(jax.random.fold_in(keys[5], 71), 0)
    teacher_head = draw_teacher_head(jax.random.fold_in(keys[5], 71), 0)
    student_hidden = draw_student_hidden(jax.random.fold_in(keys[5], 71), 0)
    student_head = draw_student_head(jax.random.fold_in(keys[5], 71), 0)
    kept = draw_kept(jax.random.fold_in(keys[5], 71), 0)
    return dict(teacher_hidden=teacher_hidden, teacher_head=teacher_head, student_hidden=student_hidden, student_head=student_head, kept=kept)


masked_value = -1e30
loss_scale = 2048.0


def reference(teacher_hidden, teacher_head, student_hidden, student_head, kept):
    block_ids = jnp.arange(NBLOCKS, dtype=jnp.int32)

    def one_block(block_number):
        row_start = (block_number * BLOCK).astype(jnp.int32)
        teacher_rows = lax.dynamic_slice_in_dim(teacher_hidden, row_start, BLOCK, 0)
        student_rows = lax.dynamic_slice_in_dim(student_hidden, row_start, BLOCK, 0)
        teacher_logits = jnp.dot(teacher_rows, teacher_head, preferred_element_type=jnp.float32)
        student_logits = jnp.dot(student_rows, student_head, preferred_element_type=jnp.float32)
        chosen = lax.dynamic_index_in_dim(kept, block_number, 0, keepdims=False)
        block_mask = jnp.any(chosen[:, None] == block_ids[None, :], axis=0)
        column_mask = jnp.repeat(block_mask, BLOCK)[None, :]
        teacher_max = jnp.max(jnp.where(column_mask, teacher_logits, masked_value), axis=1)
        weights = jnp.where(column_mask, jnp.exp(teacher_logits - teacher_max[:, None]), 0.0)
        teacher_total = jnp.sum(weights, axis=1)
        cross_total = jnp.sum(weights * student_logits, axis=1)
        self_total = jnp.sum(weights * teacher_logits, axis=1)
        student_max = jnp.max(student_logits, axis=1)
        student_exp = jnp.exp(student_logits - student_max[:, None])
        student_total = jnp.sum(student_exp, axis=1)
        loss_rows = (self_total / teacher_total - teacher_max - jnp.log(teacher_total)) - (cross_total / teacher_total - student_max - jnp.log(student_total))
        teacher_prob = weights / teacher_total[:, None]
        student_prob = student_exp / student_total[:, None]
        grad_logits = (loss_scale * (student_prob - teacher_prob)).astype(jnp.bfloat16)
        return loss_rows, grad_logits

    loss_rows, grad_logits = lax.map(one_block, jnp.arange(ROW_BLOCK_TOTAL, dtype=jnp.int32))
    grad_logits = grad_logits.reshape(TOKENS, VOCAB)
    hidden_grad = jnp.dot(grad_logits, student_head.T, preferred_element_type=jnp.float32).astype(jnp.bfloat16)
    head_grad = jnp.dot(student_hidden.T, grad_logits, preferred_element_type=jnp.float32).astype(jnp.bfloat16)
    return loss_rows.reshape(TOKENS), hidden_grad, head_grad
```

```python
import jax
import jax.numpy as jnp
from jax import lax
from jax.experimental import pallas as pl
from jax.experimental.pallas import tpu as pltpu
from jax.sharding import PartitionSpec as P

BLOCK = 128

masked_value = -1e30
loss_scale = 2048.0


def kept_kernel(ids_ref, hidden_ref, head_ref, out_ref):
    out_ref[...] = jnp.dot(
        hidden_ref[...], head_ref[...], preferred_element_type=jnp.float32
    )


def kept_partials(ids, hidden, head):
    row_blocks, slots = ids.shape
    depth = hidden.shape[1]
    return pl.pallas_call(
        kept_kernel,
        out_shape=jax.ShapeDtypeStruct((row_blocks * BLOCK, slots * BLOCK), jnp.float32),
        grid_spec=pltpu.PrefetchScalarGridSpec(
            num_scalar_prefetch=1,
            grid=(row_blocks, slots),
            in_specs=[
                pl.BlockSpec((BLOCK, depth), lambda r, m, ids: (r, 0)),
                pl.BlockSpec((depth, BLOCK), lambda r, m, ids: (0, ids[r, m])),
            ],
            out_specs=pl.BlockSpec((BLOCK, BLOCK), lambda r, m, ids: (r, m)),
        ),
        cost_estimate=pl.CostEstimate(
            flops=2 * row_blocks * slots * BLOCK * BLOCK * depth,
            bytes_accessed=2 * row_blocks * slots * BLOCK * depth,
            transcendentals=0,
        ),
        name="kept_partials",
    )(ids, hidden, head)


def body(teacher_hidden, teacher_head, student_hidden, student_head, kept):
    tokens = teacher_hidden.shape[0]
    features = student_hidden.shape[1]
    vocab_cols = teacher_head.shape[1]
    blocks_dev = vocab_cols // BLOCK
    row_blocks = tokens // BLOCK
    groups = lax.axis_size("seq")
    shards = lax.axis_size("vocab")
    seq_index = lax.axis_index("seq")
    vocab_index = lax.axis_index("vocab")
    piece_cols = vocab_cols // groups
    group_rows = tokens // groups

    def swap(value, k):
        return lax.ppermute(value, "seq", [(i, i ^ k) for i in range(groups)])

    pieces = [
        lax.dynamic_slice_in_dim(student_head, (seq_index ^ k) * piece_cols, piece_cols, 1)
        for k in range(groups)
    ]
    arrived = [pieces[0]] + [swap(pieces[k], k) for k in range(1, groups)]

    share = tokens // shards
    rows = lax.dynamic_slice_in_dim(student_hidden, vocab_index * share, share, 0)
    rows = lax.all_gather(rows, "seq", axis=0)
    rows = lax.all_gather(rows, "vocab", axis=0)

    def hidden_of(peer):
        part = lax.dynamic_index_in_dim(rows, peer, 1, False)
        return part.reshape(tokens, features)

    first_block = vocab_index * blocks_dev
    kept_count = kept.shape[1]
    slots = min(blocks_dev, max(4, kept_count // shards))
    before = jnp.sum((kept < first_block).astype(jnp.int32), axis=1)
    slot_index = before[:, None] + jnp.arange(slots, dtype=jnp.int32)[None, :]
    slot_ids = jnp.take_along_axis(kept, jnp.minimum(slot_index, kept_count - 1), axis=1)
    local_ids = slot_ids - first_block
    slot_valid = (slot_index < kept_count) & (local_ids >= 0) & (local_ids < blocks_dev)
    safe_ids = jnp.clip(local_ids, 0, blocks_dev - 1)
    partial_value = kept_partials(safe_ids, teacher_hidden, teacher_head)
    compact = lax.psum(partial_value, "seq").reshape(row_blocks, BLOCK, slots, BLOCK)
    valid = slot_valid[:, None, :, None]
    local_top = jnp.max(jnp.where(valid, compact, masked_value), axis=(2, 3))
    weights = jnp.where(valid, jnp.exp(compact - local_top[:, :, None, None]), 0.0)
    local_stats = jnp.stack(
        [local_top, jnp.sum(weights, axis=(2, 3)), jnp.sum(weights * compact, axis=(2, 3))]
    ).reshape(3, tokens)
    all_stats = lax.all_gather(local_stats, "vocab")
    teacher_max = jnp.max(all_stats[:, 0], axis=0)
    scale = jnp.exp(all_stats[:, 0] - teacher_max)
    teacher_total = jnp.sum(all_stats[:, 1] * scale, axis=0)
    self_total = jnp.sum(all_stats[:, 2] * scale, axis=0)
    top_rows = teacher_max.reshape(row_blocks, BLOCK, 1, 1)
    total_rows = teacher_total.reshape(row_blocks, BLOCK, 1, 1)
    compact_prob = jnp.where(valid, jnp.exp(compact - top_rows), 0.0) / total_rows
    aligned = piece_cols % BLOCK == 0
    my_blocks = piece_cols // BLOCK if aligned else blocks_dev
    my_first = seq_index * my_blocks if aligned else 0
    column_ids = my_first + jnp.arange(my_blocks, dtype=jnp.int32)
    placer = (
        (safe_ids[:, :, None] == column_ids[None, None, :]) & slot_valid[:, :, None]
    ).astype(jnp.float32)
    teacher_prob = jnp.einsum(
        "rtmc,rmb->rtbc", compact_prob, placer, precision=lax.Precision.HIGHEST
    ).reshape(tokens, my_blocks * BLOCK)
    if not aligned:
        teacher_prob = lax.dynamic_slice_in_dim(
            teacher_prob, seq_index * piece_cols, piece_cols, 1
        )

    student_logits = None
    for k in range(groups):
        term = jnp.dot(
            hidden_of(seq_index ^ k), arrived[k], preferred_element_type=jnp.float32
        )
        student_logits = term if student_logits is None else student_logits + term
    student_top = jnp.max(student_logits, axis=1)
    student_local = jnp.sum(jnp.exp(student_logits - student_top[:, None]), axis=1)
    cross_local = jnp.sum(teacher_prob * student_logits, axis=1)
    stats = lax.all_gather(
        jnp.stack([student_top, student_local, cross_local]), ("seq", "vocab")
    )
    student_max = jnp.max(stats[:, 0], axis=0)
    student_total = jnp.sum(stats[:, 1] * jnp.exp(stats[:, 0] - student_max), axis=0)
    cross_mean = jnp.sum(stats[:, 2], axis=0)
    loss_all = (self_total / teacher_total - teacher_max - jnp.log(teacher_total)) - (
        cross_mean - student_max - jnp.log(student_total)
    )
    loss_rows = lax.dynamic_slice_in_dim(loss_all, seq_index * group_rows, group_rows, 0)
    student_prob = jnp.exp(student_logits - student_max[:, None]) / student_total[:, None]
    grad = (loss_scale * (student_prob - teacher_prob)).astype(jnp.bfloat16)

    if groups == 4:
        half = tokens // 2
        one, two = swap(grad, 1), swap(grad, 2)
        low, high = swap(two[:half], 1), swap(one[half:], 2)
        three = jnp.concatenate([low, high], axis=0)
        grads = [grad, one, two, three]
    else:
        grads = [grad] + [swap(grad, k) for k in range(1, groups)]
    hidden_total = None
    for k in range(groups):
        term = lax.dot_general(
            grads[k], pieces[k], (((1,), (1,)), ((), ())), preferred_element_type=jnp.float32
        )
        hidden_total = term if hidden_total is None else hidden_total + term
    hidden_grad = lax.psum_scatter(hidden_total, "vocab", scatter_dimension=0, tiled=True).astype(
        jnp.bfloat16
    )
    head_grad = jnp.zeros((features, vocab_cols), jnp.bfloat16)
    for k in range(groups):
        part = lax.dot_general(
            student_hidden, grads[k], (((0,), (0,)), ((), ())), preferred_element_type=jnp.float32
        ).astype(jnp.bfloat16)
        head_grad = lax.dynamic_update_slice_in_dim(
            head_grad, part, (seq_index ^ k) * piece_cols, 1
        )
    return (loss_rows, hidden_grad, head_grad)


def solution(mesh):
    in_specs = (P(None, "seq"), P("seq", "vocab"), P(None, "seq"), P("seq", "vocab"), P())
    out_specs = (P("seq"), P("vocab", "seq"), P("seq", "vocab"))
    return jax.shard_map(body, mesh=mesh, in_specs=in_specs, out_specs=out_specs, check_vma=False)
```

```python
import jax
import jax.numpy as jnp
from jax import lax
from jax.experimental import pallas as pl
from jax.experimental.pallas import tpu as pltpu
from jax.sharding import PartitionSpec as P


BLOCK = 128

masked_value = -1e30
loss_scale = 2048.0


def kept_kernel(ids_ref, hidden_ref, head_ref, out_ref):
    out_ref[...] = jnp.dot(
        hidden_ref[...], head_ref[...], preferred_element_type=jnp.float32
    )


def kept_partials(ids, hidden, head):
    row_blocks, slots = ids.shape
    depth = hidden.shape[1]
    return pl.pallas_call(
        kept_kernel,
        out_shape=jax.ShapeDtypeStruct((row_blocks * BLOCK, slots * BLOCK), jnp.float32),
        grid_spec=pltpu.PrefetchScalarGridSpec(
            num_scalar_prefetch=1,
            grid=(row_blocks, slots),
            in_specs=[
                pl.BlockSpec((BLOCK, depth), lambda r, m, ids: (r, 0)),
                pl.BlockSpec((depth, BLOCK), lambda r, m, ids: (0, ids[r, m])),
            ],
            out_specs=pl.BlockSpec((BLOCK, BLOCK), lambda r, m, ids: (r, m)),
        ),
        cost_estimate=pl.CostEstimate(
            flops=2 * row_blocks * slots * BLOCK * BLOCK * depth,
            bytes_accessed=2 * row_blocks * slots * BLOCK * depth,
            transcendentals=0,
        ),
        name="kept_partials",
    )(ids, hidden, head)


TILE = 512


def columns_kernel(offset_ref, left_ref, right_ref, *rest):
    rest[-1][...] = jnp.dot(
        left_ref[...], right_ref[...], preferred_element_type=jnp.float32
    ).astype(jnp.bfloat16)


def put_columns(left, right, whole, cols, owner):
    rows, depth = left.shape
    part = right.shape[1]
    tiles = part // TILE
    offset = (owner * tiles).astype(jnp.int32).reshape(1)
    in_specs = [
        pl.BlockSpec((rows, depth), lambda j, o: (0, 0)),
        pl.BlockSpec((depth, TILE), lambda j, o: (0, j)),
    ]
    operands = [offset, left, right]
    aliases = {}
    if whole is not None:
        in_specs.append(pl.BlockSpec(memory_space=pl.ANY))
        operands.append(whole)
        aliases = {3: 0}
    return pl.pallas_call(
        columns_kernel,
        out_shape=jax.ShapeDtypeStruct((rows, cols), jnp.bfloat16),
        grid_spec=pltpu.PrefetchScalarGridSpec(
            num_scalar_prefetch=1,
            grid=(tiles,),
            in_specs=in_specs,
            out_specs=pl.BlockSpec((rows, TILE), lambda j, o: (0, o[0] + j)),
        ),
        input_output_aliases=aliases,
        cost_estimate=pl.CostEstimate(
            flops=2 * rows * depth * part,
            bytes_accessed=2 * (rows * depth + depth * part + rows * part),
            transcendentals=0,
        ),
        name="put_columns",
    )(*operands)


def body(teacher_hidden, teacher_head, student_hidden, student_head, kept):
    tokens = teacher_hidden.shape[0]
    features = student_hidden.shape[1]
    vocab_cols = teacher_head.shape[1]
    blocks_dev = vocab_cols // BLOCK
    row_blocks = tokens // BLOCK
    groups = lax.axis_size("seq")
    shards = lax.axis_size("vocab")
    seq_index = lax.axis_index("seq")
    vocab_index = lax.axis_index("vocab")
    piece_cols = vocab_cols // groups
    group_rows = tokens // groups

    def swap(value, k):
        return lax.ppermute(value, "seq", [(i, i ^ k) for i in range(groups)])

    pieces = [
        lax.dynamic_slice_in_dim(student_head, (seq_index ^ k) * piece_cols, piece_cols, 1)
        for k in range(groups)
    ]
    arrived = [pieces[0]] + [swap(pieces[k], k) for k in range(1, groups)]
    hidden_t = student_hidden.T

    share = tokens // shards
    rows = lax.dynamic_slice_in_dim(student_hidden, vocab_index * share, share, 0)
    rows = lax.all_gather(rows, "seq", axis=0)
    rows = lax.all_gather(rows, "vocab", axis=0)

    def hidden_of(peer):
        part = lax.dynamic_index_in_dim(rows, peer, 1, False)
        return part.reshape(tokens, features)

    first_block = vocab_index * blocks_dev
    kept_count = kept.shape[1]
    slots = min(blocks_dev, max(4, kept_count // shards))
    before = jnp.sum((kept < first_block).astype(jnp.int32), axis=1)
    slot_index = before[:, None] + jnp.arange(slots, dtype=jnp.int32)[None, :]
    slot_ids = jnp.take_along_axis(kept, jnp.minimum(slot_index, kept_count - 1), axis=1)
    local_ids = slot_ids - first_block
    slot_valid = (slot_index < kept_count) & (local_ids >= 0) & (local_ids < blocks_dev)
    safe_ids = jnp.clip(local_ids, 0, blocks_dev - 1)
    kernel_ids, hidden_t, *_ = lax.optimization_barrier((safe_ids, hidden_t, *pieces[1:]))
    partial_value = kept_partials(kernel_ids, teacher_hidden, teacher_head)
    compact = lax.psum(partial_value, "seq").reshape(row_blocks, BLOCK, slots, BLOCK)
    valid = slot_valid[:, None, :, None]
    local_top = jnp.max(jnp.where(valid, compact, masked_value), axis=(2, 3))
    weights = jnp.where(valid, jnp.exp(compact - local_top[:, :, None, None]), 0.0)
    local_stats = jnp.stack(
        [local_top, jnp.sum(weights, axis=(2, 3)), jnp.sum(weights * compact, axis=(2, 3))]
    ).reshape(3, tokens)
    all_stats = lax.all_gather(local_stats, "vocab")
    teacher_max = jnp.max(all_stats[:, 0], axis=0)
    scale = jnp.exp(all_stats[:, 0] - teacher_max)
    teacher_total = jnp.sum(all_stats[:, 1] * scale, axis=0)
    self_total = jnp.sum(all_stats[:, 2] * scale, axis=0)
    top_rows = teacher_max.reshape(row_blocks, BLOCK, 1, 1)
    total_rows = teacher_total.reshape(row_blocks, BLOCK, 1, 1)
    compact_prob = jnp.where(valid, jnp.exp(compact - top_rows), 0.0) / total_rows
    aligned = piece_cols % BLOCK == 0
    my_blocks = piece_cols // BLOCK if aligned else blocks_dev
    my_first = seq_index * my_blocks if aligned else 0
    column_ids = my_first + jnp.arange(my_blocks, dtype=jnp.int32)
    placer = (
        (safe_ids[:, :, None] == column_ids[None, None, :]) & slot_valid[:, :, None]
    ).astype(jnp.float32)
    teacher_prob = jnp.einsum(
        "rtmc,rmb->rtbc", compact_prob, placer, precision=lax.Precision.HIGHEST
    ).reshape(tokens, my_blocks * BLOCK)
    if not aligned:
        teacher_prob = lax.dynamic_slice_in_dim(
            teacher_prob, seq_index * piece_cols, piece_cols, 1
        )

    student_logits = None
    for k in range(groups):
        term = jnp.dot(
            hidden_of(seq_index ^ k), arrived[k], preferred_element_type=jnp.float32
        )
        student_logits = term if student_logits is None else student_logits + term
    student_top = jnp.max(student_logits, axis=1)
    student_local = jnp.sum(jnp.exp(student_logits - student_top[:, None]), axis=1)
    cross_local = jnp.sum(teacher_prob * student_logits, axis=1)
    stats = jnp.stack([student_top, student_local, cross_local])
    for axis in ("seq", "vocab"):
        gathered = lax.all_gather(stats, axis)
        top = jnp.max(gathered[:, 0], axis=0)
        stats = jnp.stack(
            [
                top,
                jnp.sum(gathered[:, 1] * jnp.exp(gathered[:, 0] - top), axis=0),
                jnp.sum(gathered[:, 2], axis=0),
            ]
        )
    student_max, student_total, cross_mean = stats[0], stats[1], stats[2]
    loss_all = (self_total / teacher_total - teacher_max - jnp.log(teacher_total)) - (
        cross_mean - student_max - jnp.log(student_total)
    )
    loss_rows = lax.dynamic_slice_in_dim(loss_all, seq_index * group_rows, group_rows, 0)
    student_prob = jnp.exp(student_logits - student_max[:, None]) / student_total[:, None]
    grad = (loss_scale * (student_prob - teacher_prob)).astype(jnp.bfloat16)

    if groups == 4:
        half = tokens // 2
        one, two = swap(grad, 1), swap(grad, 2)
        low = swap(two[:half], 1)
        high = swap(one[half:], 2)
        three = jnp.concatenate([low, high], axis=0)
        grads = [grad, one, two, three]
    else:
        grads = [grad] + [swap(grad, k) for k in range(1, groups)]
    hidden_total = None
    for k in range(groups):
        term = lax.dot_general(
            grads[k], pieces[k], (((1,), (1,)), ((), ())), preferred_element_type=jnp.float32
        )
        hidden_total = term if hidden_total is None else hidden_total + term
    hidden_grad = lax.psum_scatter(
        hidden_total, "vocab", scatter_dimension=0, tiled=True
    ).astype(jnp.bfloat16)
    if in_place(piece_cols):
        head_grad = None
        for k in range(groups):
            head_grad = put_columns(
                hidden_t, grads[k], head_grad, vocab_cols, seq_index ^ k
            )
        return (loss_rows, hidden_grad, head_grad)
    head_grad = jnp.zeros((features, vocab_cols), jnp.bfloat16)
    for k in range(groups):
        part = lax.dot_general(
            student_hidden, grads[k], (((0,), (0,)), ((), ())), preferred_element_type=jnp.float32
        ).astype(jnp.bfloat16)
        head_grad = lax.dynamic_update_slice_in_dim(
            head_grad, part, (seq_index ^ k) * piece_cols, 1
        )
    return (loss_rows, hidden_grad, head_grad)


def in_place(piece_cols):
    return piece_cols % TILE == 0


def solution(mesh):
    in_specs = (P(None, "seq"), P("seq", "vocab"), P(None, "seq"), P("seq", "vocab"), P())
    out_specs = (P("seq"), P("vocab", "seq"), P("seq", "vocab"))

    return jax.shard_map(body, mesh=mesh, in_specs=in_specs, out_specs=out_specs, check_vma=False)
```

```python
import jax
import jax.numpy as jnp
from jax import lax
from jax.experimental import pallas as pl
from jax.experimental.pallas import tpu as pltpu
from jax.sharding import PartitionSpec as P


BLOCK = 128

masked_value = -1e30
loss_scale = 2048.0


def kept_kernel(ids_ref, hidden_ref, head_ref, out_ref):
    out_ref[...] = jnp.dot(
        hidden_ref[...], head_ref[...], preferred_element_type=jnp.float32
    )


def kept_partials(ids, hidden, head):
    row_blocks, slots = ids.shape
    depth = hidden.shape[1]
    return pl.pallas_call(
        kept_kernel,
        out_shape=jax.ShapeDtypeStruct((row_blocks * BLOCK, slots * BLOCK), jnp.float32),
        grid_spec=pltpu.PrefetchScalarGridSpec(
            num_scalar_prefetch=1,
            grid=(row_blocks, slots),
            in_specs=[
                pl.BlockSpec((BLOCK, depth), lambda r, m, ids: (r, 0)),
                pl.BlockSpec((depth, BLOCK), lambda r, m, ids: (0, ids[r, m])),
            ],
            out_specs=pl.BlockSpec((BLOCK, BLOCK), lambda r, m, ids: (r, m)),
        ),
        cost_estimate=pl.CostEstimate(
            flops=2 * row_blocks * slots * BLOCK * BLOCK * depth,
            bytes_accessed=2 * row_blocks * slots * BLOCK * depth,
            transcendentals=0,
        ),
        name="kept_partials",
    )(ids, hidden, head)


TILE = 512


def columns_kernel(offset_ref, left_ref, right_ref, *rest):
    rest[-1][...] = jnp.dot(
        left_ref[...], right_ref[...], preferred_element_type=jnp.float32
    ).astype(jnp.bfloat16)


def put_columns(left, right, whole, cols, owner):
    rows, depth = left.shape
    part = right.shape[1]
    tiles = part // TILE
    offset = (owner * tiles).astype(jnp.int32).reshape(1)
    in_specs = [
        pl.BlockSpec((rows, depth), lambda j, o: (0, 0)),
        pl.BlockSpec((depth, TILE), lambda j, o: (0, j)),
    ]
    operands = [offset, left, right]
    aliases = {}
    if whole is not None:
        in_specs.append(pl.BlockSpec(memory_space=pl.ANY))
        operands.append(whole)
        aliases = {3: 0}
    return pl.pallas_call(
        columns_kernel,
        out_shape=jax.ShapeDtypeStruct((rows, cols), jnp.bfloat16),
        grid_spec=pltpu.PrefetchScalarGridSpec(
            num_scalar_prefetch=1,
            grid=(tiles,),
            in_specs=in_specs,
            out_specs=pl.BlockSpec((rows, TILE), lambda j, o: (0, o[0] + j)),
        ),
        input_output_aliases=aliases,
        cost_estimate=pl.CostEstimate(
            flops=2 * rows * depth * part,
            bytes_accessed=2 * (rows * depth + depth * part + rows * part),
            transcendentals=0,
        ),
        name="put_columns",
    )(*operands)


def body(teacher_hidden, teacher_head, student_hidden, student_head, kept):
    tokens = teacher_hidden.shape[0]
    features = student_hidden.shape[1]
    vocab_cols = teacher_head.shape[1]
    blocks_dev = vocab_cols // BLOCK
    row_blocks = tokens // BLOCK
    groups = lax.axis_size("seq")
    shards = lax.axis_size("vocab")
    seq_index = lax.axis_index("seq")
    vocab_index = lax.axis_index("vocab")
    piece_cols = vocab_cols // groups
    group_rows = tokens // groups

    def swap(value, k):
        return lax.ppermute(value, "seq", [(i, i ^ k) for i in range(groups)])

    pieces = [
        lax.dynamic_slice_in_dim(student_head, (seq_index ^ k) * piece_cols, piece_cols, 1)
        for k in range(groups)
    ]
    arrived = [pieces[0]] + [swap(pieces[k], k) for k in range(1, groups)]
    hidden_t = student_hidden.T

    share = tokens // shards
    rows = lax.dynamic_slice_in_dim(student_hidden, vocab_index * share, share, 0)
    rows = jnp.stack([rows] + [swap(rows, k) for k in range(1, groups)])
    rows = lax.all_gather(rows, "vocab", axis=0)

    def hidden_of(k):
        return rows[:, k].reshape(tokens, features)

    first_block = vocab_index * blocks_dev
    kept_count = kept.shape[1]
    slots = min(blocks_dev, max(4, kept_count // shards))
    before = jnp.sum((kept < first_block).astype(jnp.int32), axis=1)
    slot_index = before[:, None] + jnp.arange(slots, dtype=jnp.int32)[None, :]
    slot_ids = jnp.take_along_axis(kept, jnp.minimum(slot_index, kept_count - 1), axis=1)
    local_ids = slot_ids - first_block
    slot_valid = (slot_index < kept_count) & (local_ids >= 0) & (local_ids < blocks_dev)
    safe_ids = jnp.clip(local_ids, 0, blocks_dev - 1)
    kernel_ids, hidden_t, *_ = lax.optimization_barrier((safe_ids, hidden_t, *pieces[1:]))
    partial_value = kept_partials(kernel_ids, teacher_hidden, teacher_head)
    student_logits = None
    for k in range(groups):
        term = jnp.dot(
            hidden_of(k), arrived[k], preferred_element_type=jnp.float32
        )
        student_logits = term if student_logits is None else student_logits + term
    student_top = jnp.max(student_logits, axis=1)
    student_local = jnp.sum(jnp.exp(student_logits - student_top[:, None]), axis=1)
    stats = jnp.stack([student_top, student_local])
    for axis in ("seq", "vocab"):
        gathered = lax.all_gather(stats, axis)
        top = jnp.max(gathered[:, 0], axis=0)
        total = jnp.sum(gathered[:, 1] * jnp.exp(gathered[:, 0] - top), axis=0)
        stats = jnp.stack([top, total])
    compact, stats = lax.optimization_barrier((lax.psum(partial_value, "seq"), stats))
    student_max, student_total = stats[0], stats[1]
    compact = compact.reshape(row_blocks, BLOCK, slots, BLOCK)
    valid = slot_valid[:, None, :, None]
    local_top = jnp.max(jnp.where(valid, compact, masked_value), axis=(2, 3))
    weights = jnp.where(valid, jnp.exp(compact - local_top[:, :, None, None]), 0.0)
    local_stats = jnp.stack(
        [local_top, jnp.sum(weights, axis=(2, 3)), jnp.sum(weights * compact, axis=(2, 3))]
    ).reshape(3, tokens)
    all_stats = lax.all_gather(local_stats, "vocab")
    teacher_max = jnp.max(all_stats[:, 0], axis=0)
    scale = jnp.exp(all_stats[:, 0] - teacher_max)
    teacher_total = jnp.sum(all_stats[:, 1] * scale, axis=0)
    self_total = jnp.sum(all_stats[:, 2] * scale, axis=0)
    top_rows = teacher_max.reshape(row_blocks, BLOCK, 1, 1)
    total_rows = teacher_total.reshape(row_blocks, BLOCK, 1, 1)
    compact_prob = jnp.where(valid, jnp.exp(compact - top_rows), 0.0) / total_rows
    aligned = piece_cols % BLOCK == 0
    my_blocks = piece_cols // BLOCK if aligned else blocks_dev
    my_first = seq_index * my_blocks if aligned else 0
    column_ids = my_first + jnp.arange(my_blocks, dtype=jnp.int32)
    placer = (
        (safe_ids[:, :, None] == column_ids[None, None, :]) & slot_valid[:, :, None]
    ).astype(jnp.float32)
    teacher_prob = jnp.einsum(
        "rtmc,rmb->rtbc", compact_prob, placer, precision=lax.Precision.HIGHEST
    ).reshape(tokens, my_blocks * BLOCK)
    if not aligned:
        teacher_prob = lax.dynamic_slice_in_dim(
            teacher_prob, seq_index * piece_cols, piece_cols, 1
        )

    cross_local = jnp.sum(teacher_prob * student_logits, axis=1)
    student_prob = jnp.exp(student_logits - student_max[:, None]) / student_total[:, None]
    grad = (loss_scale * (student_prob - teacher_prob)).astype(jnp.bfloat16)

    if groups == 4:
        half = tokens // 2
        one, two = swap(grad, 1), swap(grad, 2)
        low = swap(two[:half], 1)
        high = swap(one[half:], 2)
        three = jnp.concatenate([low, high], axis=0)
        grads = [grad, one, two, three]
    else:
        grads = [grad] + [swap(grad, k) for k in range(1, groups)]
    hidden_total = None
    for k in range(groups):
        term = lax.dot_general(
            grads[k], pieces[k], (((1,), (1,)), ((), ())), preferred_element_type=jnp.float32
        )
        hidden_total = term if hidden_total is None else hidden_total + term
    hidden_total, cross_local = lax.optimization_barrier((hidden_total, cross_local))
    hidden_grad = lax.psum_scatter(
        hidden_total, "vocab", scatter_dimension=0, tiled=True
    ).astype(jnp.bfloat16)
    cross_mean = cross_local
    for axis in ("seq", "vocab"):
        cross_mean = jnp.sum(lax.all_gather(cross_mean, axis), axis=0)
    loss_all = (self_total / teacher_total - teacher_max - jnp.log(teacher_total)) - (
        cross_mean - student_max - jnp.log(student_total)
    )
    loss_rows = lax.dynamic_slice_in_dim(loss_all, seq_index * group_rows, group_rows, 0)
    if in_place(piece_cols):
        head_grad = None
        for k in range(groups):
            head_grad = put_columns(
                hidden_t, grads[k], head_grad, vocab_cols, seq_index ^ k
            )
        return (loss_rows, hidden_grad, head_grad)
    head_grad = jnp.zeros((features, vocab_cols), jnp.bfloat16)
    for k in range(groups):
        part = lax.dot_general(
            student_hidden, grads[k], (((0,), (0,)), ((), ())), preferred_element_type=jnp.float32
        ).astype(jnp.bfloat16)
        head_grad = lax.dynamic_update_slice_in_dim(
            head_grad, part, (seq_index ^ k) * piece_cols, 1
        )
    return (loss_rows, hidden_grad, head_grad)


def in_place(piece_cols):
    return piece_cols % TILE == 0


def solution(mesh):
    in_specs = (P(None, "seq"), P("seq", "vocab"), P(None, "seq"), P("seq", "vocab"), P())
    out_specs = (P("seq"), P("vocab", "seq"), P("seq", "vocab"))

    return jax.shard_map(body, mesh=mesh, in_specs=in_specs, out_specs=out_specs, check_vma=False)
```
